32 devices in a mesh: lat: 2 (over y), lon: 8 (over z, x), lev: 2 (over core).
Axes of the slice: x: 2, y: 2, z: 4, core: 2. Of those that a mesh axis runs over, the one named last changes fastest.
Arguments:
- tokens: bfloat16 [4, 12, 96, 192], P('lev', 'lat', 'lon'), may hold values from -6 to 6
- norm1_gain: float32 [192], replicated, may hold values from 0.8 to 10
- qkv_weight: bfloat16 [192, 576], replicated, may hold values from -0.4375 to 0.4375
- proj_weight: bfloat16 [192, 192], replicated, may hold values from -0.4375 to 0.4375
- earth_bias: bfloat16 [2, 2, 6, 3312], P(None, 'lat'), may hold values from -4 to 4
- norm2_gain: float32 [192], replicated, may hold values from 0.5 to 1.5
- fc1_weight: bfloat16 [192, 768], replicated, may hold values from -0.4375 to 0.4375
- fc2_weight: bfloat16 [768, 192], replicated, may hold values from -0.21875 to 0.21875
Outputs:
- blended: bfloat16 [4, 12, 96, 192], P('lev', 'lat', 'lon')
The draws below stay inside these ranges and needn't reach their ends.
All inputs are finite; a program needn't handle non-finite values.
Results may differ from the reference program's by a relative error of at most 0.008.
The reference program's roundings to bfloat16 on the way count: a program that leaves them out, or rounds other values in their place, can miss the bound.
Values may be sent and summed in bfloat16 or wider, within the bound.
A program may use at most 64 MiB of HBM per device.

```python
import jax
import jax.numpy as jnp
from jax import lax

D = 192
HEADS = 6
FF = 768
WLV = 2
WLA = 6
WLO = 12
POS = 3312
NLEV = 4
NLAT = 12
NLON = 96
NWLEV = 2
NWLAT = 2


def draw_norm1_gain(key, part):
    second_key = jax.random.fold_in(jax.random.fold_in(key, 11), 1)
    return jax.random.uniform(second_key, (D,), jnp.float32, 0.8, 1.25)


def steps_of(own_key, dims, cuts, smallest, high):
    level = 1.0
    for axis_at, parts in cuts:
        draws = jax.random.uniform(jax.random.fold_in(jax.random.fold_in(own_key, 6), axis_at), (parts,), jnp.float32, smallest / len(cuts), high / len(cuts))
        level = level * jnp.repeat(jnp.exp(draws), dims[axis_at] // parts).reshape((-1,) + (1,) * (len(dims) - 1 - axis_at))
    return level


def centred(key, shape, width, limit, shards=(), held_as=jnp.bfloat16):
    loudness = steps_of(key, shape, shards, -0.22, 0.18) if shards else 1.0
    entries = jax.random.normal(key, shape, jnp.float32) * width * loudness
    return jnp.minimum(jnp.maximum(entries, -limit), limit).astype(held_as)


def setup_inputs(seed: int = 0) -> dict:
    splits = jax.random.split(jax.random.key(seed), 9)
    return {
        "tokens": centred(splits[0], (NLEV, NLAT, NLON, D), 1.0, 6.0, ((0, 2), (1, 2), (2, 8))),
        "norm1_gain": draw_norm1_gain(jax.random.fold_in(splits[8], 71), 0),
        "qkv_weight": centred(splits[2], (D, 3 * D), D ** -0.5, 0.4375),
        "proj_weight": centred(splits[3], (D, D), D ** -0.5, 0.4375),
        "earth_bias": centred(splits[4], (NWLEV, NWLAT, HEADS, POS), 1.0, 4.0, ((1, 2),)),
        "norm2_gain": jnp.clip(1.0 + 0.1 * jax.random.normal(splits[5], (D,), jnp.float32), 0.5, 1.5),
        "fc1_weight": centred(splits[6], (D, FF), D ** -0.5, 0.4375),
        "fc2_weight": centred(splits[7], (FF, D), FF ** -0.5, 0.21875),
    }


norm_eps = 1e-05

def layer_norm(values, scale_gain):
    average = lax.optimization_barrier(jnp.mean(values, axis=-1, keepdims=True))
    centered = values - average
    variance = lax.optimization_barrier(jnp.mean(centered * centered, axis=-1, keepdims=True))
    return centered * lax.rsqrt(variance + norm_eps) * scale_gain

def window_coords():
    places = jnp.arange(WLV * WLA * WLO, dtype=jnp.int32)
    return (places // (WLA * WLO), places // WLO % WLA, places % WLO)

def bias_index():
    lev_place, lat_place, lon_place = window_coords()
    paired = (lev_place[:, None] * WLV + lev_place[None, :]) * WLA + lat_place[:, None]
    paired = paired * WLA + lat_place[None, :]
    return (paired * (2 * WLO - 1) + lon_place[:, None] - lon_place[None, :] + WLO - 1).astype(jnp.int32)

def region_of(places, extent, window):
    return jnp.where(places < extent - window, 0, jnp.where(places < extent - window // 2, 1, 2)).astype(jnp.int32)

def attend_windows(windows, qkv_weight, bias_terms, allowed):
    window_count, window_size, feature_width = windows.shape
    head_dim = feature_width // HEADS
    projected = jnp.dot(windows.reshape(window_count * window_size, feature_width), qkv_weight, preferred_element_type=jnp.float32)
    projected = lax.optimization_barrier(projected.astype(jnp.bfloat16))
    projected = projected.reshape(window_count, window_size, 3, HEADS, head_dim).astype(jnp.float32)
    queries = projected[:, :, 0]
    key_rows = projected[:, :, 1]
    value_rows = projected[:, :, 2]
    scores = jnp.einsum('wqhd,wkhd->whqk', queries, key_rows) * head_dim ** (-0.5) + bias_terms
    scores = jnp.where(allowed[:, None], scores, -1e+30)
    row_max = lax.optimization_barrier(jnp.max(scores, axis=-1, keepdims=True))
    weights = jnp.exp(scores - row_max)
    probs = weights / lax.optimization_barrier(jnp.sum(weights, axis=-1, keepdims=True))
    probs = lax.optimization_barrier(probs.astype(jnp.bfloat16))
    context = jnp.einsum('whqk,wkhd->wqhd', probs.astype(jnp.float32), value_rows)
    return context.astype(jnp.bfloat16).reshape(window_count, window_size, feature_width)

def reference(tokens, norm1_gain, qkv_weight, proj_weight, earth_bias, norm2_gain, fc1_weight, fc2_weight):
    half_lev, half_lat, half_lon = (WLV // 2, WLA // 2, WLO // 2)
    normed = layer_norm(tokens.astype(jnp.float32), norm1_gain).astype(jnp.bfloat16)
    rolled = jnp.roll(normed, (-half_lev, -half_lat, -half_lon), axis=(0, 1, 2))
    table_index = bias_index()
    lev_place, lat_place, lon_place = window_coords()
    lon_windows = NLON // WLO
    window_size = WLV * WLA * WLO

    def one_band(flat_index):
        lev_window = flat_index // NWLAT
        lat_window = flat_index % NWLAT
        zero = jnp.zeros((), jnp.int32)
        banded = lax.dynamic_slice(rolled, (lev_window * WLV, lat_window * WLA, zero, zero), (WLV, WLA, NLON, D))
        windows = banded.reshape(WLV, WLA, lon_windows, WLO, D).transpose(2, 0, 1, 3, 4)
        windows = windows.reshape(lon_windows, window_size, D)
        tables = earth_bias[lev_window, lat_window]
        bias_terms = jnp.take(tables, table_index, axis=1).astype(jnp.float32)
        lev_region = region_of(lev_window * WLV + lev_place, NLEV, WLV)
        lat_region = region_of(lat_window * WLA + lat_place, NLAT, WLA)
        allowed = (lev_region[:, None] == lev_region[None, :]) & (lat_region[:, None] == lat_region[None, :])
        context = attend_windows(windows, qkv_weight, bias_terms[None], allowed[None])
        context = context.reshape(lon_windows, WLV, WLA, WLO, D).transpose(1, 2, 0, 3, 4)
        return context.reshape(WLV, WLA, NLON, D)
    bands = lax.map(one_band, jnp.arange(NWLEV * NWLAT, dtype=jnp.int32))
    context = bands.reshape(NWLEV, NWLAT, WLV, WLA, NLON, D).transpose(0, 2, 1, 3, 4, 5)
    context = context.reshape(NLEV, NLAT, NLON, D)
    context = jnp.roll(context, (half_lev, half_lat, half_lon), axis=(0, 1, 2))

    def one_level(paired_level):
        own_level, mixed_level = paired_level
        first = own_level.reshape(-1, D).astype(jnp.float32) + jnp.dot(mixed_level.reshape(-1, D), proj_weight, preferred_element_type=jnp.float32)
        normed_two = layer_norm(first, norm2_gain).astype(jnp.bfloat16)
        hidden = jax.nn.gelu(jnp.dot(normed_two, fc1_weight, preferred_element_type=jnp.float32), approximate=False).astype(jnp.bfloat16)
        result = first + jnp.dot(hidden, fc2_weight, preferred_element_type=jnp.float32)
        return result.astype(jnp.bfloat16).reshape(own_level.shape)
    return lax.map(one_level, (tokens, context))
```

```python
import functools

import jax
import jax.numpy as jnp
import numpy as np
from jax import lax
from jax.experimental import pallas as pl
from jax.experimental.pallas import tpu as pltpu
from jax.sharding import PartitionSpec as P

HEADS = 6
WLV = 2
WLA = 6
WLO = 12
HALF_LA = WLA // 2
HALF_LO = WLO // 2
OCT = HALF_LA * HALF_LO
PLACES = WLV * WLA * WLO
HALF = PLACES // 2
SPAN = 2 * WLO - 1
CHUNK = WLA * SPAN
ROWS = 8
LANES = 128
AXES = ("lev", "lat", "lon")
BLOCK = WLO * ROWS

norm_eps = 1e-05


def octant_place(lev, lat, lon):
    octant = (lev * 2 + lat // HALF_LA) * 2 + lon // HALF_LO
    return octant * OCT + lat % HALF_LA * HALF_LO + lon % HALF_LO


def spread_matrix():
    spread = np.zeros((PLACES * ROWS, PLACES), np.float32)
    for lev in range(WLV):
        for lat in range(WLA):
            for lon in range(WLO):
                row = ((lev * WLA + lat) * WLO + lon) * ROWS
                spread[row : row + ROWS, octant_place(lev, lat, lon)] = 1
    return spread


def toeplitz_matrix():
    pick = np.zeros((CHUNK, WLO * LANES), np.float32)
    for lon in range(WLO):
        for key_lat in range(WLA):
            for key_lon in range(WLO):
                column = lon * LANES + octant_place(0, key_lat, key_lon)
                pick[key_lat * SPAN + lon - key_lon + WLO - 1, column] = 1
    return pick


def layer_norm(values, scale_gain):
    average = jnp.mean(values, axis=-1, keepdims=True)
    centered = values - average
    variance = jnp.mean(centered * centered, axis=-1, keepdims=True)
    return centered * lax.rsqrt(variance + norm_eps) * scale_gain


def bits_of(octant):
    return (octant >> 2 & 1, octant >> 1 & 1, octant & 1)


def matmul(a, b):
    return jnp.dot(a, b, preferred_element_type=jnp.float32)


def kernel(
    sizes,
    tokens_ref,
    gain1_ref,
    qkv_ref,
    proj_ref,
    table_ref,
    gain2_ref,
    fc1_ref,
    fc2_ref,
    spread_ref,
    gather_ref,
    pick_ref,
    out_ref,
    own,
    send1,
    land1,
    send2,
    land2,
    window,
    table,
    bias,
    scores,
    probs,
    mixed,
    sems,
    rows_out,
):
    where = [lax.axis_index(axis) for axis in AXES]
    features = own.shape[-1]

    def neighbour(octant, sign):
        return {
            axis: lax.rem(at + sign * step + size, size)
            for axis, at, size, step in zip(AXES, where, sizes, bits_of(octant))
        }

    barrier = pltpu.get_barrier_semaphore()
    for octant in range(1, 8):
        for sign in (-1, 1):
            pl.semaphore_signal(
                barrier,
                inc=1,
                device_id=neighbour(octant, sign),
                device_id_type=pl.DeviceIdType.MESH,
            )
    for lev in range(WLV):
        for lat in range(WLA):
            cells = tokens_ref[lev, lat].astype(jnp.float32)
            for side in range(2):
                start = octant_place(lev, lat, side * HALF_LO)
                own[start : start + HALF_LO, :] = cells[side * HALF_LO : (side + 1) * HALF_LO]
    for octant in range(7):
        send1[octant] = own[octant * OCT : (octant + 1) * OCT, :].astype(jnp.bfloat16)
    pl.semaphore_wait(barrier, 14)

    first_copies = []
    for slot in (7, 5, 3, 1, 6, 2, 4):
        copy = pltpu.make_async_remote_copy(
            src_ref=send1.at[7 - slot],
            dst_ref=land1.at[slot],
            send_sem=sems.at[0, slot],
            recv_sem=sems.at[1, slot],
            device_id=neighbour(slot, -1),
            device_id_type=pl.DeviceIdType.MESH,
        )
        copy.start()
        first_copies.append((slot, copy))

    table[...] = jnp.zeros_like(table)
    table[0:HEADS, :] = table_ref[where[0], 0].astype(jnp.float32)
    chunks = jnp.concatenate(
        [table[:, c * CHUNK : (c + 1) * CHUNK] for c in range(WLV * WLV * WLA)], axis=0
    )
    bias[...] = matmul(chunks.astype(jnp.bfloat16), pick_ref[...])

    window[0:OCT, :] = own[7 * OCT : 8 * OCT, :]
    for slot, copy in first_copies:
        copy.wait_recv()
        window[slot * OCT : (slot + 1) * OCT, :] = land1[slot].astype(jnp.float32)

    normed = layer_norm(window[...], gain1_ref[...]).astype(jnp.bfloat16)
    projected = matmul(normed, qkv_ref[...])
    queries = projected[:, :features].astype(jnp.bfloat16)

    def padded_half(values):
        zeros = jnp.zeros((LANES - HALF, features), jnp.float32)
        rows = jnp.concatenate([values[:HALF], zeros, values[HALF:], zeros], axis=0)
        return rows.astype(jnp.bfloat16)

    key_rows = padded_half(projected[:, features : 2 * features])
    value_rows = padded_half(projected[:, 2 * features :])
    row_head = lax.broadcasted_iota(jnp.int32, (PLACES * ROWS, features), 0) % ROWS
    column_head = lax.broadcasted_iota(jnp.int32, (PLACES * ROWS, features), 1) // (
        features // HEADS
    )
    head_mask = row_head == column_head
    spread = jnp.where(head_mask, matmul(spread_ref[...], queries), 0.0).astype(jnp.bfloat16)
    scores[...] = lax.dot_general(
        spread, key_rows, (((1,), (1,)), ((), ())), preferred_element_type=jnp.float32
    )

    lane = lax.broadcasted_iota(jnp.int32, (1, 2 * LANES), 1)
    key_lev = lane // LANES
    key_in = lane % LANES
    key_lat = key_in // (2 * OCT)
    last_lev = where[0] == sizes[0] - 1
    last_lat = where[1] == sizes[1] - 1
    scale = (features // HEADS) ** (-0.5)
    for lev in range(WLV):
        for lat in range(WLA):
            block = (lev * WLA + lat) * BLOCK
            terms = []
            for lon in range(WLO):
                halves = [
                    bias[
                        ((lev * WLV + side) * WLA + lat) * ROWS : ((lev * WLV + side) * WLA + lat)
                        * ROWS
                        + ROWS,
                        lon * LANES : (lon + 1) * LANES,
                    ]
                    for side in range(WLV)
                ]
                terms.append(jnp.concatenate(halves, axis=1))
            keep = key_in < HALF
            keep = keep & ((key_lev == lev) | jnp.logical_not(last_lev))
            keep = keep & ((key_lat == lat // HALF_LA) | jnp.logical_not(last_lat))
            values = scores[block : block + BLOCK, :] * scale + jnp.concatenate(terms, axis=0)
            values = jnp.where(keep, values, -1e30)
            top = jnp.max(values, axis=-1, keepdims=True)
            weights = jnp.exp(values - top)
            total = jnp.sum(weights, axis=-1, keepdims=True)
            probs[block : block + BLOCK, :] = (weights * (1.0 / total)).astype(jnp.bfloat16)

    context = matmul(probs[...], value_rows)
    context = jnp.where(head_mask, context, 0.0).astype(jnp.bfloat16)
    mixed[...] = matmul(gather_ref[...], context)
    for slot in range(1, 8):
        send2[slot] = mixed[slot * OCT : (slot + 1) * OCT, :].astype(jnp.bfloat16)

    second_copies = []
    for slot in (7, 5, 3, 1, 6, 2, 4):
        copy = pltpu.make_async_remote_copy(
            src_ref=send2.at[slot],
            dst_ref=land2.at[7 - slot],
            send_sem=sems.at[2, slot],
            recv_sem=sems.at[3, 7 - slot],
            device_id=neighbour(slot, 1),
            device_id_type=pl.DeviceIdType.MESH,
        )
        copy.start()
        second_copies.append((7 - slot, copy))

    window[7 * OCT : 8 * OCT, :] = mixed[0:OCT, :]
    for octant, copy in second_copies:
        copy.wait_recv()
        window[octant * OCT : (octant + 1) * OCT, :] = land2[octant].astype(jnp.float32)

    first = own[...] + matmul(window[...].astype(jnp.bfloat16), proj_ref[...])
    normed_two = layer_norm(first, gain2_ref[...]).astype(jnp.bfloat16)
    hidden = matmul(normed_two, fc1_ref[...])
    hidden = (0.5 * hidden * (1.0 + lax.erf(hidden * np.float32(0.5**0.5)))).astype(jnp.bfloat16)
    rows_out[...] = first + matmul(hidden, fc2_ref[...])
    for lev in range(WLV):
        for lat in range(WLA):
            for side in range(2):
                start = octant_place(lev, lat, side * HALF_LO)
                out_ref[lev, lat, side * HALF_LO : (side + 1) * HALF_LO, :] = rows_out[
                    start : start + HALF_LO, :
                ].astype(jnp.bfloat16)
    for _, copy in first_copies:
        copy.wait_send()
    for _, copy in second_copies:
        copy.wait_send()


def per_device(
    sizes,
    tokens,
    norm1_gain,
    qkv_weight,
    proj_weight,
    earth_bias,
    norm2_gain,
    fc1_weight,
    fc2_weight,
):
    assert tokens.shape[:3] == (WLV, WLA, WLO)
    features = tokens.shape[-1]
    spread = spread_matrix()
    octants = pltpu.VMEM((8, OCT, features), jnp.bfloat16)
    cells = pltpu.VMEM((PLACES, features), jnp.float32)
    operands = (
        tokens,
        norm1_gain.reshape(1, -1),
        qkv_weight,
        proj_weight,
        earth_bias,
        norm2_gain.reshape(1, -1),
        fc1_weight,
        fc2_weight,
        jnp.asarray(spread, jnp.bfloat16),
        jnp.asarray(spread.T, jnp.bfloat16),
        jnp.asarray(toeplitz_matrix(), jnp.bfloat16),
    )
    return pl.pallas_call(
        functools.partial(kernel, sizes),
        out_shape=jax.ShapeDtypeStruct(tokens.shape, jnp.bfloat16),
        in_specs=[pl.BlockSpec(memory_space=pltpu.VMEM)] * len(operands),
        out_specs=pl.BlockSpec(memory_space=pltpu.VMEM),
        scratch_shapes=[
            cells,
            octants,
            octants,
            octants,
            octants,
            cells,
            pltpu.VMEM((ROWS, earth_bias.shape[-1]), jnp.float32),
            pltpu.VMEM((WLV * WLV * WLA * ROWS, WLO * LANES), jnp.float32),
            pltpu.VMEM((PLACES * ROWS, 2 * LANES), jnp.float32),
            pltpu.VMEM((PLACES * ROWS, 2 * LANES), jnp.bfloat16),
            cells,
            pltpu.SemaphoreType.DMA((4, 8)),
            cells,
        ],
        compiler_params=pltpu.CompilerParams(
            collective_id=0, has_side_effects=True, vmem_limit_bytes=48 * 1024 * 1024
        ),
    )(*operands)


def solution(mesh):
    placed = (
        P("lev", "lat", "lon", None),
        P(),
        P(),
        P(),
        P(None, "lat", None, None),
        P(),
        P(),
        P(),
    )
    return jax.shard_map(
        functools.partial(per_device, tuple(mesh.shape[axis] for axis in AXES)),
        mesh=mesh,
        in_specs=placed,
        out_specs=P("lev", "lat", "lon", None),
        check_vma=False,
    )
```

```python
import functools

import jax
import jax.numpy as jnp
import numpy as np
from jax import lax
from jax.experimental import pallas as pl
from jax.experimental.pallas import tpu as pltpu
from jax.sharding import PartitionSpec as P

HEADS = 6
WLV = 2
WLA = 6
WLO = 12
HALF_LA = WLA // 2
HALF_LO = WLO // 2
OCT = HALF_LA * HALF_LO
PLACES = WLV * WLA * WLO
HALF = PLACES // 2
SPAN = 2 * WLO - 1
CHUNK = WLA * SPAN
ROWS = 8
LANES = 128
AXES = ("lev", "lat", "lon")
BLOCK = WLO * ROWS
OPERANDS = 11

norm_eps = 1e-05


def octant_place(lev, lat, lon):
    octant = (lev * 2 + lat // HALF_LA) * 2 + lon // HALF_LO
    return octant * OCT + lat % HALF_LA * HALF_LO + lon % HALF_LO


def spread_matrix():
    spread = np.zeros((PLACES * ROWS, PLACES), np.float32)
    for lev in range(WLV):
        for lat in range(WLA):
            for lon in range(WLO):
                row = ((lev * WLA + lat) * WLO + lon) * ROWS
                spread[row : row + ROWS, octant_place(lev, lat, lon)] = 1
    return spread


def toeplitz_matrix():
    pick = np.zeros((CHUNK, WLO * LANES), np.float32)
    for lon in range(WLO):
        for key_lat in range(WLA):
            for key_lon in range(WLO):
                column = lon * LANES + octant_place(0, key_lat, key_lon)
                pick[key_lat * SPAN + lon - key_lon + WLO - 1, column] = 1
    return pick


def layer_norm(values, scale_gain):
    average = jnp.mean(values, axis=-1, keepdims=True)
    centered = values - average
    variance = jnp.mean(centered * centered, axis=-1, keepdims=True)
    return centered * lax.rsqrt(variance + norm_eps) * scale_gain


def bits_of(octant):
    return (octant >> 2 & 1, octant >> 1 & 1, octant & 1)


def matmul(a, b):
    return jnp.dot(a, b, preferred_element_type=jnp.float32)


def kernel(sizes, *refs):
    operands, out_ref, held = refs[:OPERANDS], refs[OPERANDS], refs[OPERANDS + 1 : -14]
    (
        own,
        send1,
        land1,
        send2,
        land2,
        window,
        table,
        bias,
        scores,
        probs,
        mixed,
        sems,
        rows_out,
        load_sems,
    ) = refs[-14:]
    loads = [
        pltpu.make_async_copy(source, place, load_sems.at[i])
        for i, (source, place) in enumerate(zip(operands, held))
    ]
    for load in loads:
        load.start()
    (
        tokens_ref,
        table_ref,
        pick_ref,
        gain1_ref,
        qkv_ref,
        spread_ref,
        gather_ref,
        proj_ref,
        gain2_ref,
        fc1_ref,
        fc2_ref,
    ) = held
    where = [lax.axis_index(axis) for axis in AXES]
    features = own.shape[-1]
    count = sizes[2]
    middle = count // 2 - 1
    mine = where[2]
    my_window = jnp.where(mine < middle, mine, jnp.where(mine == middle, count - 1, mine - 1))
    keeps_slot = {0: mine < middle, 1: mine > middle}

    def worker(lon_window):
        return jnp.where(
            lon_window < middle,
            lon_window,
            jnp.where(lon_window == count - 1, middle, lon_window + 1),
        )

    def device(slot, sign, lon):
        place = {
            axis: lax.rem(at + sign * step + size, size)
            for axis, at, size, step in zip(AXES[:2], where, sizes, bits_of(slot))
        }
        place["lon"] = lon
        return place

    def window_device(slot):
        return device(slot, -1, worker(lax.rem(mine - bits_of(slot)[2] + count, count)))

    def cell_device(slot):
        return device(slot, 1, lax.rem(my_window + bits_of(slot)[2], count))

    def unless_mine(slot, action, otherwise=None):
        if slot not in keeps_slot:
            action()
            return
        pl.when(jnp.logical_not(keeps_slot[slot]))(action)
        if otherwise is not None:
            pl.when(keeps_slot[slot])(otherwise)

    barrier = pltpu.get_barrier_semaphore()
    for slot in range(8):

        def greet(slot=slot):
            for there in (window_device(slot), cell_device(slot)):
                pl.semaphore_signal(
                    barrier, inc=1, device_id=there, device_id_type=pl.DeviceIdType.MESH
                )

        unless_mine(slot, greet)
    loads[0].wait()
    for lat in range(WLA):
        for lon in range(WLO):
            cell = tokens_ref[lat, lon].astype(jnp.float32)
            for lev in range(WLV):
                place = octant_place(lev, lat, lon)
                own[place : place + 1, :] = cell[lev : lev + 1]
    for octant in range(8):
        send1[octant] = own[octant * OCT : (octant + 1) * OCT, :].astype(jnp.bfloat16)
    pl.semaphore_wait(barrier, jnp.where(mine == middle, 16, 14))

    order = (7, 5, 3, 1, 6, 4, 2, 0)
    first_copies = []
    for slot in order:
        copy = pltpu.make_async_remote_copy(
            src_ref=send1.at[7 - slot],
            dst_ref=land1.at[slot],
            send_sem=sems.at[0, slot],
            recv_sem=sems.at[1, slot],
            device_id=window_device(slot),
            device_id_type=pl.DeviceIdType.MESH,
        )

        def keep(slot=slot):
            land1[slot] = send1[7 - slot]

        unless_mine(slot, copy.start, keep)
        first_copies.append((slot, copy))

    loads[1].wait()
    loads[2].wait()
    table[...] = jnp.zeros_like(table)
    for head in range(HEADS):
        pair = table_ref[0, head].astype(jnp.float32)
        table[head : head + 1, :] = jnp.where(where[0] == 0, pair[0:1], pair[1:2])
    chunks = jnp.concatenate(
        [table[:, c * CHUNK : (c + 1) * CHUNK] for c in range(WLV * WLV * WLA)], axis=0
    )
    bias[...] = matmul(chunks.astype(jnp.bfloat16), pick_ref[...])

    for load in loads[3:]:
        load.wait()
    for slot, copy in first_copies:
        unless_mine(slot, copy.wait_recv)
        window[slot * OCT : (slot + 1) * OCT, :] = land1[slot].astype(jnp.float32)

    normed = layer_norm(window[...], gain1_ref[...]).astype(jnp.bfloat16)
    projected = matmul(normed, qkv_ref[...])
    queries = projected[:, :features].astype(jnp.bfloat16)

    def padded_half(values):
        zeros = jnp.zeros((LANES - HALF, features), jnp.float32)
        rows = jnp.concatenate([values[:HALF], zeros, values[HALF:], zeros], axis=0)
        return rows.astype(jnp.bfloat16)

    key_rows = padded_half(projected[:, features : 2 * features])
    value_rows = padded_half(projected[:, 2 * features :])
    row_head = lax.broadcasted_iota(jnp.int32, (PLACES * ROWS, features), 0) % ROWS
    column_head = lax.broadcasted_iota(jnp.int32, (PLACES * ROWS, features), 1) // (
        features // HEADS
    )
    head_mask = row_head == column_head
    spread = jnp.where(head_mask, matmul(spread_ref[...], queries), 0.0).astype(jnp.bfloat16)
    scores[...] = lax.dot_general(
        spread, key_rows, (((1,), (1,)), ((), ())), preferred_element_type=jnp.float32
    )

    lane = lax.broadcasted_iota(jnp.int32, (1, 2 * LANES), 1)
    key_lev = lane // LANES
    key_in = lane % LANES
    key_lat = key_in // (2 * OCT)
    last_lev = where[0] == sizes[0] - 1
    last_lat = where[1] == sizes[1] - 1
    scale = (features // HEADS) ** (-0.5)
    for lev in range(WLV):
        for lat in range(WLA):
            block = (lev * WLA + lat) * BLOCK
            terms = []
            for lon in range(WLO):
                halves = [
                    bias[
                        ((lev * WLV + side) * WLA + lat) * ROWS : ((lev * WLV + side) * WLA + lat)
                        * ROWS
                        + ROWS,
                        lon * LANES : (lon + 1) * LANES,
                    ]
                    for side in range(WLV)
                ]
                terms.append(jnp.concatenate(halves, axis=1))
            keep = key_in < HALF
            keep = keep & ((key_lev == lev) | jnp.logical_not(last_lev))
            keep = keep & ((key_lat == lat // HALF_LA) | jnp.logical_not(last_lat))
            values = scores[block : block + BLOCK, :] * scale + jnp.concatenate(terms, axis=0)
            values = jnp.where(keep, values, -1e30)
            top = jnp.max(values, axis=-1, keepdims=True)
            weights = jnp.exp(values - top)
            total = jnp.sum(weights, axis=-1, keepdims=True)
            probs[block : block + BLOCK, :] = (weights * (1.0 / total)).astype(jnp.bfloat16)

    context = matmul(probs[...], value_rows)
    context = jnp.where(head_mask, context, 0.0).astype(jnp.bfloat16)
    mixed[...] = matmul(gather_ref[...], context)
    for slot in range(8):
        send2[slot] = mixed[slot * OCT : (slot + 1) * OCT, :].astype(jnp.bfloat16)

    second_copies = []
    for slot in order:
        copy = pltpu.make_async_remote_copy(
            src_ref=send2.at[slot],
            dst_ref=land2.at[7 - slot],
            send_sem=sems.at[2, slot],
            recv_sem=sems.at[3, slot],
            device_id=cell_device(slot),
            device_id_type=pl.DeviceIdType.MESH,
        )

        def keep(slot=slot):
            land2[7 - slot] = send2[slot]

        unless_mine(slot, copy.start, keep)
        second_copies.append((slot, copy))

    for slot, copy in second_copies:
        unless_mine(slot, copy.wait_recv)
        octant = 7 - slot
        window[octant * OCT : (octant + 1) * OCT, :] = land2[octant].astype(jnp.float32)

    first = own[...] + matmul(window[...].astype(jnp.bfloat16), proj_ref[...])
    normed_two = layer_norm(first, gain2_ref[...]).astype(jnp.bfloat16)
    hidden = matmul(normed_two, fc1_ref[...])
    hidden = (0.5 * hidden * (1.0 + lax.erf(hidden * np.float32(0.5**0.5)))).astype(jnp.bfloat16)
    rows_out[...] = first + lax.dot_general(
        hidden, fc2_ref[...], (((1,), (1,)), ((), ())), preferred_element_type=jnp.float32
    )
    for lat in range(WLA):
        for lon in range(WLO):
            places = [octant_place(lev, lat, lon) for lev in range(WLV)]
            out_ref[lat, lon] = jnp.concatenate(
                [rows_out[place : place + 1, :] for place in places], axis=0
            ).astype(jnp.bfloat16)
    for slot, copy in first_copies + second_copies:
        unless_mine(slot, copy.wait_send)


def per_device(
    sizes,
    tokens,
    norm1_gain,
    qkv_weight,
    proj_weight,
    earth_bias,
    norm2_gain,
    fc1_weight,
    fc2_weight,
):
    assert tokens.shape[:3] == (WLV, WLA, WLO)
    features = tokens.shape[-1]
    spread = spread_matrix()
    octants = pltpu.VMEM((8, OCT, features), jnp.bfloat16)
    cells = pltpu.VMEM((PLACES, features), jnp.float32)
    operands = (
        tokens.transpose(1, 2, 0, 3),
        earth_bias.transpose(1, 2, 0, 3),
        jnp.asarray(toeplitz_matrix(), jnp.bfloat16),
        norm1_gain.reshape(1, -1),
        qkv_weight,
        jnp.asarray(spread, jnp.bfloat16),
        jnp.asarray(spread.T, jnp.bfloat16),
        proj_weight,
        norm2_gain.reshape(1, -1),
        fc1_weight,
        fc2_weight.T,
    )
    assert len(operands) == OPERANDS
    blended = pl.pallas_call(
        functools.partial(kernel, sizes),
        out_shape=jax.ShapeDtypeStruct(operands[0].shape, jnp.bfloat16),
        in_specs=[pl.BlockSpec(memory_space=pltpu.HBM)] * OPERANDS,
        out_specs=pl.BlockSpec(memory_space=pltpu.VMEM),
        scratch_shapes=[
            *[pltpu.VMEM(operand.shape, operand.dtype) for operand in operands],
            cells,
            octants,
            octants,
            octants,
            octants,
            cells,
            pltpu.VMEM((ROWS, earth_bias.shape[-1]), jnp.float32),
            pltpu.VMEM((WLV * WLV * WLA * ROWS, WLO * LANES), jnp.float32),
            pltpu.VMEM((PLACES * ROWS, 2 * LANES), jnp.float32),
            pltpu.VMEM((PLACES * ROWS, 2 * LANES), jnp.bfloat16),
            cells,
            pltpu.SemaphoreType.DMA((4, 8)),
            cells,
            pltpu.SemaphoreType.DMA((OPERANDS,)),
        ],
        compiler_params=pltpu.CompilerParams(
            collective_id=0, has_side_effects=True, vmem_limit_bytes=67_043_328
        ),
    )(*operands)
    return blended.transpose(2, 0, 1, 3)


def solution(mesh):
    placed = (
        P("lev", "lat", "lon", None),
        P(),
        P(),
        P(),
        P(None, "lat", None, None),
        P(),
        P(),
        P(),
    )
    return jax.shard_map(
        functools.partial(per_device, tuple(mesh.shape[axis] for axis in AXES)),
        mesh=mesh,
        in_specs=placed,
        out_specs=P("lev", "lat", "lon", None),
        check_vma=False,
    )
```

```python
import functools

import jax
import jax.numpy as jnp
import numpy as np
from jax import lax
from jax.experimental import pallas as pl
from jax.experimental.pallas import tpu as pltpu
from jax.sharding import PartitionSpec as P

HEADS = 6
WLV = 2
WLA = 6
WLO = 12
HALF_LA = WLA // 2
HALF_LO = WLO // 2
OCT = HALF_LA * HALF_LO
PLACES = WLV * WLA * WLO
HALF = PLACES // 2
SPAN = 2 * WLO - 1
CHUNK = WLA * SPAN
ROWS = 8
LANES = 128
AXES = ("lev", "lat", "lon")
BLOCK = WLO * ROWS
OPERANDS = 11

norm_eps = 1e-05


def octant_place(lev, lat, lon):
    octant = (lev * 2 + lat // HALF_LA) * 2 + lon // HALF_LO
    return octant * OCT + lat % HALF_LA * HALF_LO + lon % HALF_LO


def spread_matrix():
    spread = np.zeros((PLACES * ROWS, PLACES), np.float32)
    for lev in range(WLV):
        for lat in range(WLA):
            for lon in range(WLO):
                row = ((lev * WLA + lat) * WLO + lon) * ROWS
                spread[row : row + ROWS, octant_place(lev, lat, lon)] = 1
    return spread


def toeplitz_matrix():
    pick = np.zeros((CHUNK, WLO * LANES), np.float32)
    for lon in range(WLO):
        for key_lat in range(WLA):
            for key_lon in range(WLO):
                column = lon * LANES + octant_place(0, key_lat, key_lon)
                pick[key_lat * SPAN + lon - key_lon + WLO - 1, column] = 1
    return pick


def layer_norm(values, scale_gain):
    average = jnp.mean(values, axis=-1, keepdims=True)
    centered = values - average
    variance = jnp.mean(centered * centered, axis=-1, keepdims=True)
    return centered * lax.rsqrt(variance + norm_eps) * scale_gain


def window_workers(count):
    middle = count // 2 - 1
    if count % 4:
        low = list(range(middle))
        return low + list(range(middle + 1, count)) + [middle]
    low = [w ^ 1 for w in range(middle - 1)] + [middle - 1]
    high = [w + 2 if w % 2 else w for w in range(middle, count - 1)]
    return low + high + [middle]


def bits_of(octant):
    return (octant >> 2 & 1, octant >> 1 & 1, octant & 1)


def matmul(a, b):
    return jnp.dot(a, b, preferred_element_type=jnp.float32)


def kernel(sizes, *refs):
    operands, out_ref, held = refs[:OPERANDS], refs[OPERANDS], refs[OPERANDS + 1 : -14]
    (
        own,
        send1,
        land1,
        send2,
        land2,
        window,
        table,
        bias,
        scores,
        probs,
        mixed,
        sems,
        rows_out,
        load_sems,
    ) = refs[-14:]
    loads = [
        pltpu.make_async_copy(source, place, load_sems.at[i])
        for i, (source, place) in enumerate(zip(operands, held))
    ]
    for load in loads:
        load.start()
    (
        tokens_ref,
        table_ref,
        pick_ref,
        gain1_ref,
        qkv_ref,
        spread_ref,
        gather_ref,
        proj_ref,
        gain2_ref,
        fc1_ref,
        fc2_ref,
    ) = held
    where = [lax.axis_index(axis) for axis in AXES]
    features = own.shape[-1]
    count = sizes[2]
    mine = where[2]
    workers = window_workers(count)

    def entry(values, index):
        found = jnp.int32(values[0])
        for i, value in enumerate(values[1:], 1):
            found = jnp.where(index == i, value, found)
        return found

    my_window = entry([workers.index(i) for i in range(count)], mine)
    keeps_slot = {0: my_window == mine, 1: lax.rem(my_window + 1, count) == mine}
    keeps_none = jnp.logical_not(keeps_slot[0] | keeps_slot[1])

    def worker(lon_window):
        return entry(workers, lon_window)

    def device(slot, sign, lon):
        place = {
            axis: lax.rem(at + sign * step + size, size)
            for axis, at, size, step in zip(AXES[:2], where, sizes, bits_of(slot))
        }
        place["lon"] = lon
        return place

    def window_device(slot):
        return device(slot, -1, worker(lax.rem(mine - bits_of(slot)[2] + count, count)))

    def cell_device(slot):
        return device(slot, 1, lax.rem(my_window + bits_of(slot)[2], count))

    def unless_mine(slot, action, otherwise=None):
        if slot not in keeps_slot:
            action()
            return
        pl.when(jnp.logical_not(keeps_slot[slot]))(action)
        if otherwise is not None:
            pl.when(keeps_slot[slot])(otherwise)

    barrier = pltpu.get_barrier_semaphore()
    for slot in range(8):

        def greet(slot=slot):
            for there in (window_device(slot), cell_device(slot)):
                pl.semaphore_signal(
                    barrier, inc=1, device_id=there, device_id_type=pl.DeviceIdType.MESH
                )

        unless_mine(slot, greet)
    loads[0].wait()
    for lat in range(WLA):
        for lon in range(WLO):
            cell = tokens_ref[lat, lon].astype(jnp.float32)
            for lev in range(WLV):
                place = octant_place(lev, lat, lon)
                own[place : place + 1, :] = cell[lev : lev + 1]
    loads[3].wait()
    window[...] = layer_norm(own[...], gain1_ref[...])
    for octant in range(8):
        send1[octant] = window[octant * OCT : (octant + 1) * OCT, :].astype(jnp.bfloat16)
    pl.semaphore_wait(barrier, jnp.where(keeps_none, 16, 14))

    order = (7, 5, 3, 1, 6, 4, 2, 0)
    first_copies = []
    for slot in order:
        copy = pltpu.make_async_remote_copy(
            src_ref=send1.at[7 - slot],
            dst_ref=land1.at[slot],
            send_sem=sems.at[0, slot],
            recv_sem=sems.at[1, slot],
            device_id=window_device(slot),
            device_id_type=pl.DeviceIdType.MESH,
        )

        def keep(slot=slot):
            land1[slot] = send1[7 - slot]

        unless_mine(slot, copy.start, keep)
        first_copies.append((slot, copy))

    loads[1].wait()
    loads[2].wait()
    table[...] = jnp.zeros_like(table)
    for head in range(HEADS):
        pair = table_ref[0, head].astype(jnp.float32)
        table[head : head + 1, :] = jnp.where(where[0] == 0, pair[0:1], pair[1:2])
    chunks = jnp.concatenate(
        [table[:, c * CHUNK : (c + 1) * CHUNK] for c in range(WLV * WLV * WLA)], axis=0
    )
    bias[...] = matmul(chunks.astype(jnp.bfloat16), pick_ref[...])

    for load in loads[4:]:
        load.wait()
    for slot, copy in first_copies:
        unless_mine(slot, copy.wait_recv)
        window[slot * OCT : (slot + 1) * OCT, :] = land1[slot].astype(jnp.float32)

    normed = window[...].astype(jnp.bfloat16)
    projected = matmul(normed, qkv_ref[...])
    queries = projected[:, :features].astype(jnp.bfloat16)

    def padded_half(values):
        zeros = jnp.zeros((LANES - HALF, features), jnp.float32)
        rows = jnp.concatenate([values[:HALF], zeros, values[HALF:], zeros], axis=0)
        return rows.astype(jnp.bfloat16)

    key_rows = padded_half(projected[:, features : 2 * features])
    value_rows = padded_half(projected[:, 2 * features :])
    row_head = lax.broadcasted_iota(jnp.int32, (ROWS, features), 0)
    column_head = lax.broadcasted_iota(jnp.int32, (ROWS, features), 1) // (features // HEADS)
    own_head = (row_head == column_head)[None]

    def of_own_head(values):
        tiles = values.reshape(PLACES, ROWS, features)
        return jnp.where(own_head, tiles, 0.0).reshape(values.shape).astype(jnp.bfloat16)

    spread = of_own_head(matmul(spread_ref[...], queries))
    scores[...] = lax.dot_general(
        spread, key_rows, (((1,), (1,)), ((), ())), preferred_element_type=jnp.float32
    )

    lane = lax.broadcasted_iota(jnp.int32, (1, 2 * LANES), 1)
    key_lev = lane // LANES
    key_in = lane % LANES
    key_lat = key_in // (2 * OCT)
    last_lev = where[0] == sizes[0] - 1
    last_lat = where[1] == sizes[1] - 1
    scale = (features // HEADS) ** (-0.5)
    for lev in range(WLV):
        for lat in range(WLA):
            block = (lev * WLA + lat) * BLOCK
            terms = []
            for lon in range(WLO):
                halves = [
                    bias[
                        ((lev * WLV + side) * WLA + lat) * ROWS : ((lev * WLV + side) * WLA + lat)
                        * ROWS
                        + ROWS,
                        lon * LANES : (lon + 1) * LANES,
                    ]
                    for side in range(WLV)
                ]
                terms.append(jnp.concatenate(halves, axis=1))
            keep = key_in < HALF
            keep = keep & ((key_lev == lev) | jnp.logical_not(last_lev))
            keep = keep & ((key_lat == lat // HALF_LA) | jnp.logical_not(last_lat))
            values = scores[block : block + BLOCK, :] * scale + jnp.concatenate(terms, axis=0)
            values = jnp.where(keep, values, -1e30)
            top = jnp.max(values, axis=-1, keepdims=True)
            weights = jnp.exp(values - top)
            total = jnp.sum(weights, axis=-1, keepdims=True)
            probs[block : block + BLOCK, :] = (weights * (1.0 / total)).astype(jnp.bfloat16)

    context = of_own_head(matmul(probs[...], value_rows))
    mixed[...] = matmul(gather_ref[...], context)
    for slot in range(8):
        send2[slot] = mixed[slot * OCT : (slot + 1) * OCT, :].astype(jnp.bfloat16)

    second_copies = []
    for slot in order:
        copy = pltpu.make_async_remote_copy(
            src_ref=send2.at[slot],
            dst_ref=land2.at[7 - slot],
            send_sem=sems.at[2, slot],
            recv_sem=sems.at[3, slot],
            device_id=cell_device(slot),
            device_id_type=pl.DeviceIdType.MESH,
        )

        def keep(slot=slot):
            land2[7 - slot] = send2[slot]

        unless_mine(slot, copy.start, keep)
        second_copies.append((slot, copy))

    for slot, copy in second_copies:
        unless_mine(slot, copy.wait_recv)
        octant = 7 - slot
        window[octant * OCT : (octant + 1) * OCT, :] = land2[octant].astype(jnp.float32)

    first = own[...] + matmul(window[...].astype(jnp.bfloat16), proj_ref[...])
    normed_two = layer_norm(first, gain2_ref[...]).astype(jnp.bfloat16)
    hidden = matmul(normed_two, fc1_ref[...])
    hidden = (0.5 * hidden * (1.0 + lax.erf(hidden * np.float32(0.5**0.5)))).astype(jnp.bfloat16)
    rows_out[...] = first + lax.dot_general(
        hidden, fc2_ref[...], (((1,), (1,)), ((), ())), preferred_element_type=jnp.float32
    )
    for lat in range(WLA):
        for lon in range(WLO):
            places = [octant_place(lev, lat, lon) for lev in range(WLV)]
            out_ref[lat, lon] = jnp.concatenate(
                [rows_out[place : place + 1, :] for place in places], axis=0
            ).astype(jnp.bfloat16)
    for slot, copy in first_copies + second_copies:
        unless_mine(slot, copy.wait_send)


def per_device(
    sizes,
    tokens,
    norm1_gain,
    qkv_weight,
    proj_weight,
    earth_bias,
    norm2_gain,
    fc1_weight,
    fc2_weight,
):
    assert tokens.shape[:3] == (WLV, WLA, WLO)
    features = tokens.shape[-1]
    spread = spread_matrix()
    octants = pltpu.VMEM((8, OCT, features), jnp.bfloat16)
    cells = pltpu.VMEM((PLACES, features), jnp.float32)
    operands = (
        tokens.transpose(1, 2, 0, 3),
        earth_bias.transpose(1, 2, 0, 3),
        jnp.asarray(toeplitz_matrix(), jnp.bfloat16),
        norm1_gain.reshape(1, -1),
        qkv_weight,
        jnp.asarray(spread, jnp.bfloat16),
        jnp.asarray(spread.T, jnp.bfloat16),
        proj_weight,
        norm2_gain.reshape(1, -1),
        fc1_weight,
        fc2_weight.T,
    )
    assert len(operands) == OPERANDS
    blended = pl.pallas_call(
        functools.partial(kernel, sizes),
        out_shape=jax.ShapeDtypeStruct(operands[0].shape, jnp.bfloat16),
        in_specs=[pl.BlockSpec(memory_space=pltpu.HBM)] * OPERANDS,
        out_specs=pl.BlockSpec(memory_space=pltpu.VMEM),
        scratch_shapes=[
            *[pltpu.VMEM(operand.shape, operand.dtype) for operand in operands],
            cells,
            octants,
            octants,
            octants,
            octants,
            cells,
            pltpu.VMEM((ROWS, earth_bias.shape[-1]), jnp.float32),
            pltpu.VMEM((WLV * WLV * WLA * ROWS, WLO * LANES), jnp.float32),
            pltpu.VMEM((PLACES * ROWS, 2 * LANES), jnp.float32),
            pltpu.VMEM((PLACES * ROWS, 2 * LANES), jnp.bfloat16),
            cells,
            pltpu.SemaphoreType.DMA((4, 8)),
            cells,
            pltpu.SemaphoreType.DMA((OPERANDS,)),
        ],
        compiler_params=pltpu.CompilerParams(
            collective_id=0, has_side_effects=True, vmem_limit_bytes=67_043_328
        ),
    )(*operands)
    return blended.transpose(2, 0, 1, 3)


def solution(mesh):
    placed = (
        P("lev", "lat", "lon", None),
        P(),
        P(),
        P(),
        P(None, "lat", None, None),
        P(),
        P(),
        P(),
    )
    return jax.shard_map(
        functools.partial(per_device, tuple(mesh.shape[axis] for axis in AXES)),
        mesh=mesh,
        in_specs=placed,
        out_specs=P("lev", "lat", "lon", None),
        check_vma=False,
    )
```

```python
import functools

import jax
import jax.numpy as jnp
import numpy as np
from jax import lax
from jax.experimental import pallas as pl
from jax.experimental.pallas import tpu as pltpu
from jax.sharding import PartitionSpec as P

HEADS = 6
WLV = 2
WLA = 6
WLO = 12
HALF_LA = WLA // 2
HALF_LO = WLO // 2
OCT = HALF_LA * HALF_LO
PLACES = WLV * WLA * WLO
HALF = PLACES // 2
SPAN = 2 * WLO - 1
CHUNK = WLA * SPAN
ROWS = 8
LANES = 128
AXES = ("lev", "lat", "lon")
BLOCK = WLO * ROWS
OPERANDS = 11

norm_eps = 1e-05


def octant_place(lev, lat, lon):
    octant = (lev * 2 + lat // HALF_LA) * 2 + lon // HALF_LO
    return octant * OCT + lat % HALF_LA * HALF_LO + lon % HALF_LO


def spread_matrix():
    spread = np.zeros((PLACES * ROWS, PLACES), np.float32)
    for lev in range(WLV):
        for lat in range(WLA):
            for lon in range(WLO):
                row = ((lev * WLA + lat) * WLO + lon) * ROWS
                spread[row : row + ROWS, octant_place(lev, lat, lon)] = 1
    return spread


def toeplitz_matrix():
    pick = np.zeros((CHUNK, WLO * LANES), np.float32)
    for lon in range(WLO):
        for key_lat in range(WLA):
            for key_lon in range(WLO):
                column = lon * LANES + octant_place(0, key_lat, key_lon)
                pick[key_lat * SPAN + lon - key_lon + WLO - 1, column] = 1
    return pick


def layer_norm(values, scale_gain):
    average = jnp.mean(values, axis=-1, keepdims=True)
    centered = values - average
    variance = jnp.mean(centered * centered, axis=-1, keepdims=True)
    return centered * lax.rsqrt(variance + norm_eps) * scale_gain


def window_workers(count):
    middle = count // 2 - 1
    if count % 4:
        low = list(range(middle))
        return low + list(range(middle + 1, count)) + [middle]
    low = [w ^ 1 for w in range(middle - 1)] + [middle - 1]
    high = [w + 2 if w % 2 else w for w in range(middle, count - 1)]
    return low + high + [middle]


def bits_of(octant):
    return (octant >> 2 & 1, octant >> 1 & 1, octant & 1)


def matmul(a, b):
    return jnp.dot(a, b, preferred_element_type=jnp.float32)


def kernel(sizes, *refs):
    operands, out_ref, held = refs[:OPERANDS], refs[OPERANDS], refs[OPERANDS + 1 : -14]
    (
        own,
        send1,
        land1,
        send2,
        land2,
        window,
        table,
        bias,
        scores,
        probs,
        mixed,
        sems,
        rows_out,
        load_sems,
    ) = refs[-14:]
    loads = [
        pltpu.make_async_copy(source, place, load_sems.at[i])
        for i, (source, place) in enumerate(zip(operands, held))
    ]
    for load in loads:
        load.start()
    (
        tokens_ref,
        table_ref,
        pick_ref,
        gain1_ref,
        qkv_ref,
        spread_ref,
        gather_ref,
        proj_ref,
        gain2_ref,
        fc1_ref,
        fc2_ref,
    ) = held
    where = [lax.axis_index(axis) for axis in AXES]
    features = own.shape[-1]
    count = sizes[2]
    mine = where[2]
    workers = window_workers(count)

    def entry(values, index):
        found = jnp.int32(values[0])
        for i, value in enumerate(values[1:], 1):
            found = jnp.where(index == i, value, found)
        return found

    my_window = entry([workers.index(i) for i in range(count)], mine)
    keeps_slot = {0: my_window == mine, 1: lax.rem(my_window + 1, count) == mine}
    keeps_none = jnp.logical_not(keeps_slot[0] | keeps_slot[1])

    def worker(lon_window):
        return entry(workers, lon_window)

    def device(slot, sign, lon):
        place = {
            axis: lax.rem(at + sign * step + size, size)
            for axis, at, size, step in zip(AXES[:2], where, sizes, bits_of(slot))
        }
        place["lon"] = lon
        return place

    def window_device(slot):
        return device(slot, -1, worker(lax.rem(mine - bits_of(slot)[2] + count, count)))

    def cell_device(slot):
        return device(slot, 1, lax.rem(my_window + bits_of(slot)[2], count))

    def unless_mine(slot, action, otherwise=None):
        if slot not in keeps_slot:
            action()
            return
        pl.when(jnp.logical_not(keeps_slot[slot]))(action)
        if otherwise is not None:
            pl.when(keeps_slot[slot])(otherwise)

    barrier = pltpu.get_barrier_semaphore()
    for slot in range(8):

        def greet(slot=slot):
            for there in (window_device(slot), cell_device(slot)):
                pl.semaphore_signal(
                    barrier, inc=1, device_id=there, device_id_type=pl.DeviceIdType.MESH
                )

        unless_mine(slot, greet)
    loads[0].wait()
    for lat in range(WLA):
        for lon in range(WLO):
            cell = tokens_ref[lat, lon].astype(jnp.float32)
            for lev in range(WLV):
                place = octant_place(lev, lat, lon)
                own[place : place + 1, :] = cell[lev : lev + 1]
    loads[3].wait()
    window[...] = layer_norm(own[...], gain1_ref[...])
    for octant in range(8):
        send1[octant] = window[octant * OCT : (octant + 1) * OCT, :].astype(jnp.bfloat16)
    pl.semaphore_wait(barrier, jnp.where(keeps_none, 16, 14))

    order = (7, 5, 3, 1, 6, 4, 2, 0)
    first_copies = []
    for slot in order:
        copy = pltpu.make_async_remote_copy(
            src_ref=send1.at[7 - slot],
            dst_ref=land1.at[slot],
            send_sem=sems.at[0, slot],
            recv_sem=sems.at[1, slot],
            device_id=window_device(slot),
            device_id_type=pl.DeviceIdType.MESH,
        )

        def keep(slot=slot):
            land1[slot] = send1[7 - slot]

        unless_mine(slot, copy.start, keep)
        first_copies.append((slot, copy))

    loads[1].wait()
    loads[2].wait()
    table[...] = jnp.zeros_like(table)
    for head in range(HEADS):
        pair = table_ref[0, head].astype(jnp.float32)
        table[head : head + 1, :] = jnp.where(where[0] == 0, pair[0:1], pair[1:2])
    chunks = jnp.concatenate(
        [table[:, c * CHUNK : (c + 1) * CHUNK] for c in range(WLV * WLV * WLA)], axis=0
    )
    bias[...] = matmul(chunks.astype(jnp.bfloat16), pick_ref[...])

    for load in loads[4:]:
        load.wait()
    for slot, copy in first_copies:
        unless_mine(slot, copy.wait_recv)
        window[slot * OCT : (slot + 1) * OCT, :] = land1[slot].astype(jnp.float32)

    normed = window[...].astype(jnp.bfloat16)
    projected = matmul(normed, qkv_ref[...])
    queries = projected[:, :features].astype(jnp.bfloat16)

    def padded_half(values):
        zeros = jnp.zeros((LANES - HALF, features), jnp.float32)
        rows = jnp.concatenate([values[:HALF], zeros, values[HALF:], zeros], axis=0)
        return rows.astype(jnp.bfloat16)

    key_rows = padded_half(projected[:, features : 2 * features])
    value_rows = padded_half(projected[:, 2 * features :])
    row_head = lax.broadcasted_iota(jnp.int32, (ROWS, features), 0)
    column_head = lax.broadcasted_iota(jnp.int32, (ROWS, features), 1) // (features // HEADS)
    own_head = (row_head == column_head)[None]

    def of_own_head(values):
        tiles = values.reshape(PLACES, ROWS, features)
        return jnp.where(own_head, tiles, 0.0).reshape(values.shape).astype(jnp.bfloat16)

    spread = of_own_head(matmul(spread_ref[...], queries))
    scores[...] = lax.dot_general(
        spread, key_rows, (((1,), (1,)), ((), ())), preferred_element_type=jnp.float32
    )

    lane = lax.broadcasted_iota(jnp.int32, (1, 2 * LANES), 1)
    key_lev = lane // LANES
    key_in = lane % LANES
    key_lat = key_in // (2 * OCT)
    last_lev = where[0] == sizes[0] - 1
    last_lat = where[1] == sizes[1] - 1
    scale = (features // HEADS) ** (-0.5)
    for lev in range(WLV):
        for lat in range(WLA):
            block = (lev * WLA + lat) * BLOCK
            terms = []
            for lon in range(WLO):
                halves = [
                    bias[
                        ((lev * WLV + side) * WLA + lat) * ROWS : ((lev * WLV + side) * WLA + lat)
                        * ROWS
                        + ROWS,
                        lon * LANES : (lon + 1) * LANES,
                    ]
                    for side in range(WLV)
                ]
                terms.append(jnp.concatenate(halves, axis=1))
            keep = key_in < HALF
            keep = keep & ((key_lev == lev) | jnp.logical_not(last_lev))
            keep = keep & ((key_lat == lat // HALF_LA) | jnp.logical_not(last_lat))
            values = scores[block : block + BLOCK, :] * scale + jnp.concatenate(terms, axis=0)
            values = jnp.where(keep, values, -1e30)
            top = jnp.max(values, axis=-1, keepdims=True)
            weights = jnp.exp(values - top)
            total = jnp.sum(weights, axis=-1, keepdims=True)
            probs[block : block + BLOCK, :] = (weights * (1.0 / total)).astype(jnp.bfloat16)

    context = of_own_head(matmul(probs[...], value_rows))
    mixed[...] = matmul(gather_ref[...], context)
    for slot in range(8):
        send2[slot] = mixed[slot * OCT : (slot + 1) * OCT, :].astype(jnp.bfloat16)

    second_copies = []
    for slot in order:
        copy = pltpu.make_async_remote_copy(
            src_ref=send2.at[slot],
            dst_ref=land2.at[7 - slot],
            send_sem=sems.at[2, slot],
            recv_sem=sems.at[3, slot],
            device_id=cell_device(slot),
            device_id_type=pl.DeviceIdType.MESH,
        )

        def keep(slot=slot):
            land2[7 - slot] = send2[slot]

        unless_mine(slot, copy.start, keep)
        second_copies.append((slot, copy))

    for slot, copy in second_copies:
        unless_mine(slot, copy.wait_recv)
        octant = 7 - slot
        window[octant * OCT : (octant + 1) * OCT, :] = land2[octant].astype(jnp.float32)

    first = own[...] + matmul(window[...].astype(jnp.bfloat16), proj_ref[...])
    normed_two = layer_norm(first, gain2_ref[...]).astype(jnp.bfloat16)
    hidden = matmul(normed_two, fc1_ref[...])
    hidden = (0.5 * hidden * (1.0 + lax.erf(hidden * np.float32(0.5**0.5)))).astype(jnp.bfloat16)
    rows_out[...] = first + lax.dot_general(
        hidden, fc2_ref[...], (((1,), (1,)), ((), ())), preferred_element_type=jnp.float32
    )
    for lat in range(WLA):
        for lon in range(WLO):
            places = [octant_place(lev, lat, lon) for lev in range(WLV)]
            out_ref[lat, lon] = jnp.concatenate(
                [rows_out[place : place + 1, :] for place in places], axis=0
            ).astype(jnp.bfloat16)
    for slot, copy in first_copies + second_copies:
        unless_mine(slot, copy.wait_send)


def per_device(
    sizes,
    tokens,
    norm1_gain,
    qkv_weight,
    proj_weight,
    earth_bias,
    norm2_gain,
    fc1_weight,
    fc2_weight,
):
    assert tokens.shape[:3] == (WLV, WLA, WLO)
    features = tokens.shape[-1]
    spread = spread_matrix()
    octants = pltpu.VMEM((8, OCT, features), jnp.bfloat16)
    cells = pltpu.VMEM((PLACES, features), jnp.float32)
    operands = (
        tokens.transpose(1, 2, 0, 3),
        earth_bias.transpose(1, 2, 0, 3),
        jnp.asarray(toeplitz_matrix(), jnp.bfloat16),
        norm1_gain.reshape(1, -1),
        qkv_weight,
        jnp.asarray(spread, jnp.bfloat16),
        jnp.asarray(spread.T, jnp.bfloat16),
        proj_weight,
        norm2_gain.reshape(1, -1),
        fc1_weight,
        fc2_weight.T,
    )
    assert len(operands) == OPERANDS
    blended = pl.pallas_call(
        functools.partial(kernel, sizes),
        out_shape=jax.ShapeDtypeStruct(operands[0].shape, jnp.bfloat16),
        in_specs=[pl.BlockSpec(memory_space=pltpu.HBM)] * OPERANDS,
        out_specs=pl.BlockSpec(memory_space=pltpu.VMEM),
        scratch_shapes=[
            *[pltpu.VMEM(operand.shape, operand.dtype) for operand in operands],
            cells,
            octants,
            octants,
            octants,
            octants,
            cells,
            pltpu.VMEM((ROWS, earth_bias.shape[-1]), jnp.float32),
            pltpu.VMEM((WLV * WLV * WLA * ROWS, WLO * LANES), jnp.float32),
            pltpu.VMEM((PLACES * ROWS, 2 * LANES), jnp.float32),
            pltpu.VMEM((PLACES * ROWS, 2 * LANES), jnp.bfloat16),
            cells,
            pltpu.SemaphoreType.DMA((4, 8)),
            cells,
            pltpu.SemaphoreType.DMA((OPERANDS,)),
        ],
        compiler_params=pltpu.CompilerParams(
            collective_id=0, has_side_effects=True, vmem_limit_bytes=48 * 1024 * 1024
        ),
    )(*[pltpu.with_memory_space_constraint(x, pltpu.HBM) for x in operands])
    return blended.transpose(2, 0, 1, 3)


def solution(mesh):
    placed = (
        P("lev", "lat", "lon", None),
        P(),
        P(),
        P(),
        P(None, "lat", None, None),
        P(),
        P(),
        P(),
    )
    return jax.shard_map(
        functools.partial(per_device, tuple(mesh.shape[axis] for axis in AXES)),
        mesh=mesh,
        in_specs=placed,
        out_specs=P("lev", "lat", "lon", None),
        check_vma=False,
    )
```
